32 devices in a mesh: gx: 2 (over y), gy: 4 (over x, core), gz: 4 (over z).
Axes of the slice: x: 2, y: 2, z: 4, core: 2. Of those that a mesh axis runs over, the one named last changes fastest.
Arguments:
- preact: bfloat16 [4096, 12288], P('gx', 'gy'), may hold values from -6 to 6
- grad_output: bfloat16 [4096, 4608], P(('gx', 'gy'), 'gz'), may hold values from -1.5 to 1.5
- down_weight: bfloat16 [12288, 4608], P('gy', 'gz'), may hold values from -0.09375 to 0.09375
Outputs:
- grad_pre: bfloat16 [4096, 12288], P(('gx', 'gz'), 'gy')
- grad_down: bfloat16 [12288, 4608], P(('gy', 'gx'), 'gz')
The draws below stay inside these ranges and needn't reach their ends.
All inputs are finite; a program needn't handle non-finite values.
Results may differ from the reference program's by a relative error of at most 0.013.
Values may be sent and summed in bfloat16 or wider, within the bound.
A program may use at most 256 MiB of HBM per device.

```python
import math
import jax
import jax.numpy as jnp
from jax import lax

D = 4608
FF = 12288
ROW_BLOCK = 2048
ROWS = 4096
N_GX = 2
N_GZ = 4


def steps_of(stream_key, dims, split, smallest, top_value):
    loudness = 1.0
    for position, parts in split:
        heights = jax.random.uniform(jax.random.fold_in(jax.random.fold_in(stream_key, 6), position), (parts,), jnp.float32, smallest / len(split), top_value / len(split))
        loudness = loudness * jnp.repeat(jnp.exp(heights), dims[position] // parts).reshape((-1,) + (1,) * (len(dims) - 1 - position))
    return loudness


def centred(own_key, extent, scale, limit, shards=(), kind=jnp.bfloat16):
    drawn = scale * jax.random.normal(own_key, extent, jnp.float32)
    if shards:
        drawn = drawn * steps_of(own_key, extent, shards, -0.22, 0.18)
    return jnp.clip(drawn, -limit, limit).astype(kind)


def setup_inputs(seed: int = 0) -> dict:
    key_of = jax.random.split(jax.random.key(seed), 4)
    preact = centred(key_of[0], (ROWS, FF), 1.0, 6.0, ((0, 2), (1, 4)))
    grad_output = centred(key_of[1], (ROWS, D), 0.25, 1.5, ((0, 8), (1, 4)))
    down_weight = centred(key_of[2], (FF, D), D ** -0.5, 0.09375, ((0, 4), (1, 4)))
    return {"preact": preact, "grad_output": grad_output, "down_weight": down_weight}


root_half = 1.0 / math.sqrt(2.0)
slope_scale = 1.0 / math.sqrt(2.0 * math.pi)

def gaussian_unit(values):
    return 0.5 * values * (1.0 + lax.erf(values * root_half))

def unit_slope(values):
    return 0.5 * (1.0 + lax.erf(values * root_half)) + values * jnp.exp(-0.5 * values * values) * slope_scale

def reference(preact, grad_output, down_weight):
    pre_wide = preact.astype(jnp.float32)
    activation = gaussian_unit(pre_wide).astype(jnp.bfloat16)
    feature_block = D // N_GZ
    contract_cols = (((1,), (1,)), ((), ()))

    def add_part(carry, index):
        start = (index * feature_block).astype(jnp.int32)
        out_cols = lax.dynamic_slice_in_dim(grad_output, start, feature_block, 1)
        weight_cols = lax.dynamic_slice_in_dim(down_weight, start, feature_block, 1)
        part = lax.dot_general(out_cols, weight_cols, contract_cols, preferred_element_type=jnp.float32).astype(jnp.bfloat16)
        part = lax.optimization_barrier(part)
        return (carry + part.astype(jnp.float32), None)
    grad_act, unused = lax.scan(add_part, jnp.zeros((ROWS, FF), jnp.float32), jnp.arange(N_GZ, dtype=jnp.int32))
    grad_pre = (grad_act * unit_slope(pre_wide)).astype(jnp.bfloat16)
    blocks = (activation.reshape(N_GX, ROW_BLOCK, FF), grad_output.reshape(N_GX, ROW_BLOCK, D))

    def accumulate(carry, block):
        act_block, output_block = block
        down_term = jnp.dot(act_block.T, output_block, preferred_element_type=jnp.float32).astype(jnp.bfloat16)
        down_term = lax.optimization_barrier(down_term)
        return (carry + down_term.astype(jnp.float32), None)
    down_sum, unused2 = lax.scan(accumulate, jnp.zeros((FF, D), jnp.float32), blocks)
    return (grad_pre, down_sum.astype(jnp.bfloat16))
```

```python
import math

import jax
import jax.numpy as jnp
from jax import lax
from jax.sharding import PartitionSpec as P

root_half = 1.0 / math.sqrt(2.0)
slope_scale = 1.0 / math.sqrt(2.0 * math.pi)
BF = jnp.bfloat16
F32 = jnp.float32


def unit_slope(values):
    return (
        0.5 * (1.0 + lax.erf(values * root_half))
        + values * jnp.exp(-0.5 * values * values) * slope_scale
    )


def gelu(pre):
    wide = pre.astype(F32)
    return (0.5 * wide * (1.0 + lax.erf(wide * root_half))).astype(BF)


def dot_cols(a, b):
    return lax.dot_general(a, b, (((1,), (1,)), ((), ())), preferred_element_type=F32)


def dot_rows(a, b):
    return lax.dot_general(a, b, (((0,), (0,)), ((), ())), preferred_element_type=F32)


def gather_gy(block):
    j = lax.axis_index("gy")
    rows = block.shape[0]
    flip = lambda bit: [(i, i ^ bit) for i in range(4)]
    near = lax.ppermute(block, "gy", flip(1))
    across = lax.ppermute(block, "gy", flip(2))
    far = lax.ppermute(across, "gy", flip(1))
    whole = jnp.zeros((4 * rows, block.shape[1]), block.dtype)
    for bits, part in ((0, block), (1, near), (2, across), (3, far)):
        whole = lax.dynamic_update_slice_in_dim(whole, part, (j ^ bits) * rows, 0)
    return whole


def grad_down_of(activation, output_rows):
    n_gx = lax.axis_size("gx")
    hidden = activation.shape[1]
    if n_gx != 2:
        return lax.psum_scatter(
            dot_rows(activation, output_rows).astype(BF), "gx", scatter_dimension=0, tiled=True
        )
    g = lax.axis_index("gx")
    half = hidden // 2
    pieces = 2
    size = half // pieces
    arrived = []
    for p in range(pieces):
        act = lax.dynamic_slice_in_dim(activation, (1 - g) * half + p * size, size, 1)
        term = dot_rows(act, output_rows).astype(BF)
        arrived.append(lax.ppermute(term, "gx", [(0, 1), (1, 0)]))
    out = []
    for p in range(pieces):
        act = lax.dynamic_slice_in_dim(activation, g * half + p * size, size, 1)
        term = dot_rows(act, output_rows)
        out.append((term + arrived[p].astype(F32)).astype(BF))
    return jnp.concatenate(out, 0)


def shards(preact, grad_output, down_weight):
    n_gx = lax.axis_size("gx")
    z = lax.axis_index("gz")
    g = lax.axis_index("gx")
    share_rows = preact.shape[0] // 4
    hidden = down_weight.shape[0]
    inward = [(0, 1), (3, 2)]
    outward = [(1, 0), (2, 3)]
    middle = [(1, 2), (2, 1)]

    first = hidden // 4
    half = (hidden - first) // 2
    spare = g % 2
    col_start = [0, first + spare * half, first + (1 - spare) * half]
    col_size = [first, half, half]
    weights = [lax.dynamic_slice_in_dim(down_weight, s, n, 0) for s, n in zip(col_start, col_size)]

    end_block = lax.ppermute(grad_output, "gz", inward)
    weight_mine = lax.ppermute(weights[1], "gz", inward)
    if n_gx == 2:
        weight_theirs = lax.ppermute(weight_mine, "gx", [(0, 1), (1, 0)])
    else:
        weight_theirs = lax.ppermute(weights[2], "gz", inward)
    end_weights = [None, weight_mine, weight_theirs]

    output_rows = gather_gy(grad_output)
    end_rows = gather_gy(end_block)

    def rows_of(array, mirrored):
        share = jnp.where(z >= 2, 3 - mirrored, mirrored)
        return lax.dynamic_slice_in_dim(array, share * share_rows, share_rows, 0)

    def part(mirrored, c):
        return dot_cols(rows_of(output_rows, mirrored), weights[c])

    def end_part(mirrored, c):
        if c == 0:
            return lax.ppermute(part(mirrored, 0).astype(BF), "gz", inward).astype(F32)
        return dot_cols(rows_of(end_rows, mirrored), end_weights[c])

    arrived = {}
    for c in range(3):
        for mirrored in (3, 2):
            total = (part(mirrored, c) + end_part(mirrored, c)).astype(BF)
            arrived[c, 3 - mirrored] = lax.ppermute(total, "gz", middle)

    activation = gelu(preact)
    grad_down = grad_down_of(activation, output_rows)

    pre_share = lax.dynamic_slice_in_dim(preact, z * share_rows, share_rows, 0)
    own_rows = lax.dynamic_slice_in_dim(output_rows, z * share_rows, share_rows, 0)
    own_end = lax.dynamic_slice_in_dim(end_rows, z * share_rows, share_rows, 0)
    chunks = []
    for c in range(3):
        outer = (arrived[c, 0].astype(F32) + part(0, c)).astype(BF)
        outer = lax.ppermute(outer, "gz", outward).astype(F32)
        total = dot_cols(own_rows, weights[c])
        if c == 0:
            total = total + end_part(1, 0)
        else:
            total = total + dot_cols(own_end, end_weights[c])
        total = total + arrived[c, 1].astype(F32) + outer
        pre = lax.dynamic_slice_in_dim(pre_share, col_start[c], col_size[c], 1).astype(F32)
        chunks.append((total * unit_slope(pre)).astype(BF))
    low = jnp.where(spare == 0, chunks[1], chunks[2])
    high = jnp.where(spare == 0, chunks[2], chunks[1])
    grad_pre = jnp.concatenate([chunks[0], low, high], 1)
    return (grad_pre, grad_down)


def solution(mesh):
    return jax.shard_map(
        shards,
        mesh=mesh,
        in_specs=(P("gx", "gy"), P(("gx", "gy"), "gz"), P("gy", "gz")),
        out_specs=(P(("gx", "gz"), "gy"), P(("gy", "gx"), "gz")),
        check_vma=False,
    )
```

```python
import math

import jax
import jax.numpy as jnp
from jax import lax
from jax.sharding import PartitionSpec as P

root_half = 1.0 / math.sqrt(2.0)
slope_scale = 1.0 / math.sqrt(2.0 * math.pi)
BF = jnp.bfloat16
F32 = jnp.float32


def unit_slope(values):
    return (
        0.5 * (1.0 + lax.erf(values * root_half))
        + values * jnp.exp(-0.5 * values * values) * slope_scale
    )


def gelu(pre):
    wide = pre.astype(F32)
    return (0.5 * wide * (1.0 + lax.erf(wide * root_half))).astype(BF)


def dot_cols(a, b):
    return lax.dot_general(a, b, (((1,), (1,)), ((), ())), preferred_element_type=F32)


def dot_rows(a, b):
    return lax.dot_general(a, b, (((0,), (0,)), ((), ())), preferred_element_type=F32)


def gather_gy(block):
    j = lax.axis_index("gy")
    rows = block.shape[0]
    flip = lambda bit: [(i, i ^ bit) for i in range(4)]
    near = lax.ppermute(block, "gy", flip(1))
    across = lax.ppermute(block, "gy", flip(2))
    far = lax.ppermute(across, "gy", flip(1))
    whole = jnp.zeros((4 * rows, block.shape[1]), block.dtype)
    for bits, part in ((0, block), (1, near), (2, across), (3, far)):
        whole = lax.dynamic_update_slice_in_dim(whole, part, (j ^ bits) * rows, 0)
    return whole


def after(value, *ready):
    return lax.optimization_barrier((value, *ready))[0]


def shards(preact, grad_output, down_weight):
    n_gx = lax.axis_size("gx")
    z = lax.axis_index("gz")
    g = lax.axis_index("gx")
    share_rows = preact.shape[0] // 4
    hidden = down_weight.shape[0]
    inward = [(0, 1), (3, 2)]
    outward = [(1, 0), (2, 3)]
    middle = [(1, 2), (2, 1)]
    swap = [(0, 1), (1, 0)]

    first = hidden // 4
    half = (hidden - first) // 2
    spare = g % 2
    mine, theirs = first + spare * half, first + (1 - spare) * half
    early = half // 3
    col_start = [0, mine, theirs, mine + early, theirs + early]
    col_size = [first, early, early, half - early, half - early]
    n_chunks = len(col_size)
    weights = [lax.dynamic_slice_in_dim(down_weight, s, n, 0) for s, n in zip(col_start, col_size)]

    output_rows = gather_gy(grad_output)
    end_block = lax.ppermute(grad_output, "gz", inward)
    end_rows = gather_gy(end_block)

    def rows_of(array, mirrored):
        share = jnp.where(z >= 2, 3 - mirrored, mirrored)
        return lax.dynamic_slice_in_dim(array, share * share_rows, share_rows, 0)

    def part(mirrored, c):
        return dot_cols(rows_of(output_rows, mirrored), weights[c])

    from_end = {}
    from_end[3] = lax.ppermute(part(3, 0).astype(BF), "gz", inward)
    from_end[2] = lax.ppermute(after(part(2, 0).astype(BF), from_end[3]), "gz", inward)
    end_weights = [None] * n_chunks
    last = from_end[2]
    for c in (1, 3):
        end_weights[c] = last = lax.ppermute(after(weights[c], last), "gz", inward)
        if n_gx == 2:
            end_weights[c + 1] = lax.ppermute(end_weights[c], "gx", swap)
        else:
            end_weights[c + 1] = last = lax.ppermute(after(weights[c + 1], last), "gz", inward)
    from_end[1] = lax.ppermute(after(part(1, 0).astype(BF), last), "gz", inward)

    def end_part(mirrored, c):
        if c == 0:
            return from_end[mirrored].astype(F32)
        return dot_cols(rows_of(end_rows, mirrored), end_weights[c])

    sent = []
    arrived = {}
    for c in range(n_chunks):
        for mirrored in (3, 2):
            total = (part(mirrored, c) + end_part(mirrored, c)).astype(BF)
            if c == n_chunks - 1 and mirrored == 2:
                total = after(total, sent[-1])
            elif len(sent) >= 2:
                total = after(total, sent[-2])
            arrived[c, 3 - mirrored] = lax.ppermute(total, "gz", middle)
            sent.append(arrived[c, 3 - mirrored])

    activation = gelu(preact)
    if n_gx == 2:
        pieces = 4
        size = hidden // 2 // pieces
        waits = [(), (), (end_weights[2],), (end_weights[4],)]
        down = []
        for p in range(pieces):
            act = lax.dynamic_slice_in_dim(activation, (1 - g) * (hidden // 2) + p * size, size, 1)
            term = after(dot_rows(act, output_rows).astype(BF), *waits[p])
            down.append(lax.ppermute(term, "gx", swap))
        for p in range(pieces):
            act = lax.dynamic_slice_in_dim(activation, g * (hidden // 2) + p * size, size, 1)
            down[p] = (dot_rows(act, output_rows) + down[p].astype(F32)).astype(BF)
        grad_down = jnp.concatenate(down, 0)
    else:
        grad_down = lax.psum_scatter(
            dot_rows(activation, output_rows).astype(BF), "gx", scatter_dimension=0, tiled=True
        )

    pre_share = lax.dynamic_slice_in_dim(preact, z * share_rows, share_rows, 0)
    own_rows = lax.dynamic_slice_in_dim(output_rows, z * share_rows, share_rows, 0)
    own_end = lax.dynamic_slice_in_dim(end_rows, z * share_rows, share_rows, 0)
    chunks = []
    for c in range(n_chunks):
        outer = (arrived[c, 0].astype(F32) + part(0, c)).astype(BF)
        outer = lax.ppermute(outer, "gz", outward).astype(F32)
        total = dot_cols(own_rows, weights[c])
        if c == 0:
            total = total + end_part(1, 0)
        else:
            total = total + dot_cols(own_end, end_weights[c])
        total = total + arrived[c, 1].astype(F32) + outer
        pre = lax.dynamic_slice_in_dim(pre_share, col_start[c], col_size[c], 1).astype(F32)
        chunks.append((total * unit_slope(pre)).astype(BF))
    pick = lambda a, b: [jnp.where(spare == 0, chunks[a + i], chunks[b + i]) for i in (0, 2)]
    grad_pre = jnp.concatenate([chunks[0], *pick(1, 2), *pick(2, 1)], 1)
    return (grad_pre, grad_down)


def solution(mesh):
    return jax.shard_map(
        shards,
        mesh=mesh,
        in_specs=(P("gx", "gy"), P(("gx", "gy"), "gz"), P("gy", "gz")),
        out_specs=(P(("gx", "gz"), "gy"), P(("gy", "gx"), "gz")),
        check_vma=False,
    )
```

```python
import math

import jax
import jax.numpy as jnp
from jax import lax
from jax.sharding import PartitionSpec as P

root_half = 1.0 / math.sqrt(2.0)
slope_scale = 1.0 / math.sqrt(2.0 * math.pi)
BF = jnp.bfloat16
F32 = jnp.float32


def unit_slope(values):
    return (
        0.5 * (1.0 + lax.erf(values * root_half))
        + values * jnp.exp(-0.5 * values * values) * slope_scale
    )


def gelu(pre):
    wide = pre.astype(F32)
    return (0.5 * wide * (1.0 + lax.erf(wide * root_half))).astype(BF)


def dot_cols(a, b):
    return lax.dot_general(a, b, (((1,), (1,)), ((), ())), preferred_element_type=F32)


def dot_rows(a, b):
    return lax.dot_general(a, b, (((0,), (0,)), ((), ())), preferred_element_type=F32)


def gather_gy(block):
    j = lax.axis_index("gy")
    rows = block.shape[0]
    flip = lambda bit: [(i, i ^ bit) for i in range(4)]
    near = lax.ppermute(block, "gy", flip(1))
    across = lax.ppermute(block, "gy", flip(2))
    far = lax.ppermute(across, "gy", flip(1))
    whole = jnp.zeros((4 * rows, block.shape[1]), block.dtype)
    for bits, part in ((0, block), (1, near), (2, across), (3, far)):
        whole = lax.dynamic_update_slice_in_dim(whole, part, (j ^ bits) * rows, 0)
    return whole


def after(value, *ready):
    return lax.optimization_barrier((value, *ready))[0]


def shards(preact, grad_output, down_weight):
    n_gx = lax.axis_size("gx")
    z = lax.axis_index("gz")
    g = lax.axis_index("gx")
    share_rows = preact.shape[0] // 4
    hidden = down_weight.shape[0]
    inward = [(0, 1), (3, 2)]
    outward = [(1, 0), (2, 3)]
    middle = [(1, 2), (2, 1)]
    swap = [(0, 1), (1, 0)]

    first = hidden // 4
    half = (hidden - first) // 2
    spare = g % 2
    mine, theirs = first + spare * half, first + (1 - spare) * half
    early = half // 3
    col_start = [0, mine, theirs, mine + early, theirs + early]
    col_size = [first, early, early, half - early, half - early]
    n_chunks = len(col_size)
    weights = [lax.dynamic_slice_in_dim(down_weight, s, n, 0) for s, n in zip(col_start, col_size)]

    output_rows = gather_gy(grad_output)
    end_block = lax.ppermute(grad_output, "gz", inward)
    end_rows = gather_gy(end_block)

    def rows_of(array, mirrored):
        share = jnp.where(z >= 2, 3 - mirrored, mirrored)
        return lax.dynamic_slice_in_dim(array, share * share_rows, share_rows, 0)

    def part(mirrored, c):
        return dot_cols(rows_of(output_rows, mirrored), weights[c])

    from_end = {}
    from_end[3] = lax.ppermute(part(3, 0).astype(BF), "gz", inward)
    from_end[2] = lax.ppermute(part(2, 0).astype(BF), "gz", inward)
    end_weights = [None] * n_chunks
    last = from_end[3]
    for c in (1, 3):
        end_weights[c] = last = lax.ppermute(after(weights[c], last), "gz", inward)
        if n_gx == 2:
            end_weights[c + 1] = lax.ppermute(end_weights[c], "gx", swap)
        else:
            end_weights[c + 1] = last = lax.ppermute(after(weights[c + 1], last), "gz", inward)
    from_end[1] = lax.ppermute(after(part(1, 0).astype(BF), last), "gz", inward)

    def end_part(mirrored, c):
        if c == 0:
            return from_end[mirrored].astype(F32)
        return dot_cols(rows_of(end_rows, mirrored), end_weights[c])

    sent = []
    arrived = {}
    for c in range(n_chunks):
        for mirrored in (3, 2):
            total = (part(mirrored, c) + end_part(mirrored, c)).astype(BF)
            if c == n_chunks - 1 and mirrored == 2:
                total = after(total, sent[-1])
            elif len(sent) >= 2:
                total = after(total, sent[-2])
            arrived[c, 3 - mirrored] = lax.ppermute(total, "gz", middle)
            sent.append(arrived[c, 3 - mirrored])

    activation = gelu(preact)
    if n_gx == 2:
        pieces = 4
        size = hidden // 2 // pieces
        waits = [(), (), (end_weights[2],), (end_weights[4],)]
        down = []
        for p in range(pieces):
            act = lax.dynamic_slice_in_dim(activation, (1 - g) * (hidden // 2) + p * size, size, 1)
            term = after(dot_rows(act, output_rows).astype(BF), *waits[p])
            down.append(lax.ppermute(term, "gx", swap))
        for p in range(pieces):
            act = lax.dynamic_slice_in_dim(activation, g * (hidden // 2) + p * size, size, 1)
            down[p] = (dot_rows(act, output_rows) + down[p].astype(F32)).astype(BF)
        grad_down = jnp.concatenate(down, 0)
    else:
        grad_down = lax.psum_scatter(
            dot_rows(activation, output_rows).astype(BF), "gx", scatter_dimension=0, tiled=True
        )

    pre_share = lax.dynamic_slice_in_dim(preact, z * share_rows, share_rows, 0)
    own_rows = lax.dynamic_slice_in_dim(output_rows, z * share_rows, share_rows, 0)
    own_end = lax.dynamic_slice_in_dim(end_rows, z * share_rows, share_rows, 0)
    chunks = []
    for c in range(n_chunks):
        outer = (arrived[c, 0].astype(F32) + part(0, c)).astype(BF)
        outer = lax.ppermute(outer, "gz", outward).astype(F32)
        total = dot_cols(own_rows, weights[c])
        if c == 0:
            total = total + end_part(1, 0)
        else:
            total = total + dot_cols(own_end, end_weights[c])
        total = total + arrived[c, 1].astype(F32) + outer
        pre = lax.dynamic_slice_in_dim(pre_share, col_start[c], col_size[c], 1).astype(F32)
        chunks.append((total * unit_slope(pre)).astype(BF))
    pick = lambda a, b: [jnp.where(spare == 0, chunks[a + i], chunks[b + i]) for i in (0, 2)]
    grad_pre = jnp.concatenate([chunks[0], *pick(1, 2), *pick(2, 1)], 1)
    return (grad_pre, grad_down)


def solution(mesh):
    return jax.shard_map(
        shards,
        mesh=mesh,
        in_specs=(P("gx", "gy"), P(("gx", "gy"), "gz"), P("gy", "gz")),
        out_specs=(P(("gx", "gz"), "gy"), P(("gy", "gx"), "gz")),
        check_vma=False,
    )
```
